32 devices in a mesh: groups: 2 (over x), blk: 16 (over z, y, core).
Axes of the slice: x: 2, y: 2, z: 4, core: 2. Of those that a mesh axis runs over, the one named last changes fastest.
Arguments:
- query: bfloat16 [8192, 1024], P(('groups', 'blk')), parts along dimension 0, may hold values from -5 to 5
- key_in: bfloat16 [8192, 1024], P(('groups', 'blk')), parts along dimension 0, may hold values from -6 to 6
- value: bfloat16 [8192, 1024], P(('groups', 'blk')), parts along dimension 0, may hold values from -6 to 6
- grad_out: bfloat16 [8192, 1024], P(('groups', 'blk')), parts along dimension 0, may hold values from -6 to 6
- neighbors: int32 [64, 8], P(('groups', 'blk')), parts along dimension 0, may hold values from 0 to 31, as said below
- counts: int32 [64], P(('groups', 'blk')), parts along dimension 0, may hold values from 2 to 8, as said below
Outputs:
- attn_out: bfloat16 [8192, 1024], P(('groups', 'blk')), parts along dimension 0
- grad_query: bfloat16 [8192, 1024], P(('groups', 'blk')), parts along dimension 0
- grad_key: bfloat16 [8192, 1024], P(('groups', 'blk')), parts along dimension 0
- grad_value: bfloat16 [8192, 1024], P(('groups', 'blk')), parts along dimension 0
The draws below stay inside these ranges and needn't reach their ends.
There are 2 independent parts, one for each index of `groups`. The reference program is written for one: setup_inputs(seed, part) draws one part's arguments, and reference() takes and returns one part's arrays. A program takes and returns all parts, laid end to end along the dimension named above; each array names one. Nothing has to cross between parts.
Inputs may be any that keep to these rules, and one draw needn't show every extreme that they name: `neighbors`: row b holds 8 distinct block indices; its first entry is b itself; every entry is a block whose device (block // 2) is at most 2 steps from b's device along blk, counted cyclically; only the first counts[b] entries are used. `counts`: some block has exactly 8 and some exactly 2.
All inputs are finite; a program needn't handle non-finite values.
Results may differ from the reference program's by a relative error of at most 0.0086.
Values may be sent and summed in bfloat16 or wider, within the bound.
No kernel may reach another device: no remote copies, remote signals or barrier semaphores. Data moves between devices by JAX's collectives and lax.ppermute only.
A program may use at most 128 MiB of HBM per device.

```python
import math
import jax
import jax.numpy as jnp
from jax import lax

HEADS = 16
HDIM = 64
D = 1024
BLOCK = 128
BLK_DEV = 2
NB = 8
REACH = 2
BLOCKS = 32
NODES = 4096


def draw_query(key, part):
    model_width = HEADS * HDIM
    entries = jnp.clip(jax.random.normal(jax.random.fold_in(key, 1), (NODES, model_width), jnp.float32), -5.0, 5.0)
    return entries.astype(jnp.bfloat16)


def draw_key_in(key, part):
    model_width = HEADS * HDIM
    entries = jnp.clip(jax.random.normal(jax.random.fold_in(key, 3), (NODES, model_width), jnp.float32), -6.0, 6.0)
    return entries.astype(jnp.bfloat16)


def draw_neighbors(key, part):
    shard_count = BLOCKS // BLK_DEV
    span_blocks = (2 * REACH + 1) * BLK_DEV
    block_ids = jnp.arange(BLOCKS)
    home = block_ids // BLK_DEV
    window_ids = jnp.arange(span_blocks)
    window_blocks = jnp.mod(home[:, None] - REACH + window_ids[None, :] // BLK_DEV, shard_count) * BLK_DEV + window_ids[None, :] % BLK_DEV
    own_slot = REACH * BLK_DEV + block_ids % BLK_DEV
    ranking = jax.random.randint(jax.random.fold_in(key, 11), (BLOCKS, span_blocks), 0, 1 << 20) * span_blocks + window_ids[None, :]
    ranking = jnp.where(window_ids[None, :] == own_slot[:, None], -1, ranking)
    picked = jnp.argsort(ranking, axis=1)[:, :NB]
    return jnp.take_along_axis(window_blocks, picked, axis=1).astype(jnp.int32)


def draw_counts(key, part):
    shard_count = BLOCKS // BLK_DEV
    block_ids = jnp.arange(BLOCKS)
    base = jax.random.randint(jax.random.fold_in(key, 21), (BLOCKS,), 2, NB + 1)
    heavy = jax.random.randint(jax.random.fold_in(key, 22), (shard_count,), 0, 8) == 0
    base = jnp.where(jnp.repeat(heavy, BLK_DEV), NB, base)
    fullest = jax.random.randint(jax.random.fold_in(key, 23), (), 0, BLOCKS)
    lowest = jnp.mod(fullest + 1 + jax.random.randint(jax.random.fold_in(key, 24), (), 0, BLOCKS - 1), BLOCKS)
    base = jnp.where(block_ids == fullest, NB, base)
    base = jnp.where(block_ids == lowest, 2, base)
    return base.astype(jnp.int32)


def steps_of(key, dims, pieces, least, high):
    gain = 1.0
    for axis_at, shards_of in pieces:
        draws = jax.random.uniform(jax.random.fold_in(jax.random.fold_in(key, 6), axis_at), (shards_of,), jnp.float32, least / len(pieces), high / len(pieces))
        gain = gain * jnp.repeat(jnp.exp(draws), dims[axis_at] // shards_of).reshape((-1,) + (1,) * (len(dims) - 1 - axis_at))
    return gain


def normal_values(stream_key, dims, width, bound, shards=(), held_as=jnp.bfloat16):
    factor_of = steps_of(stream_key, dims, shards, -0.22, 0.18) if shards else 1.0
    values = jax.random.normal(stream_key, dims, jnp.float32) * width * factor_of
    return jnp.minimum(jnp.maximum(values, -bound), bound).astype(held_as)


def setup_inputs(seed: int = 0, part: int = 0) -> dict:
    splits = jax.random.split(jax.random.key(seed), 7)
    part_splits = jax.random.split(jax.random.fold_in(splits[6], part), 7)
    query = draw_query(jax.random.fold_in(jax.random.fold_in(splits[6], part), 71), part)
    key_in = draw_key_in(jax.random.fold_in(jax.random.fold_in(splits[6], part), 71), part)
    value = normal_values(part_splits[2], (NODES, D), 1.0, 6.0, ((0, 16),))
    grad_out = normal_values(part_splits[3], (NODES, D), 1.0, 6.0, ((0, 16),))
    neighbors = draw_neighbors(jax.random.fold_in(jax.random.fold_in(splits[6], part), 71), part)
    counts = draw_counts(jax.random.fold_in(jax.random.fold_in(splits[6], part), 71), part)
    return dict(query=query, key_in=key_in, value=value, grad_out=grad_out, neighbors=neighbors, counts=counts)


def split_heads(matrix):
    return matrix.reshape(matrix.shape[0], HEADS, HDIM).astype(jnp.float32)

def merge_heads(matrix):
    return matrix.reshape(matrix.shape[0], HEADS * HDIM)

def reference(query, key_in, value, grad_out, neighbors, counts):
    factor = 1.0 / math.sqrt(HDIM)
    model_width = HEADS * HDIM
    q_blocks = query.reshape(BLOCKS, BLOCK, model_width)
    k_blocks = key_in.reshape(BLOCKS, BLOCK, model_width)
    v_blocks = value.reshape(BLOCKS, BLOCK, model_width)
    g_blocks = grad_out.reshape(BLOCKS, BLOCK, model_width)
    slot_ids = jnp.arange(NB, dtype=jnp.int32)

    def block_tiles(blk_id):
        chosen = neighbors[blk_id]
        k_all = split_heads(k_blocks[chosen].reshape(NB * BLOCK, model_width))
        v_all = split_heads(v_blocks[chosen].reshape(NB * BLOCK, model_width))
        live_keys = jnp.repeat(slot_ids < counts[blk_id], BLOCK)
        q_tile = split_heads(q_blocks[blk_id])
        scores = jnp.einsum('qhd,khd->hqk', q_tile, k_all) * factor
        scores = jnp.where(live_keys[None, None, :], scores, -jnp.inf)
        row_max = lax.optimization_barrier(jnp.max(scores, axis=2, keepdims=True))
        exponent = jnp.exp(scores - row_max)
        soft_probs = exponent / lax.optimization_barrier(jnp.sum(exponent, axis=2, keepdims=True))
        rounded = lax.optimization_barrier(soft_probs.astype(jnp.bfloat16)).astype(jnp.float32)
        return (chosen, q_tile, k_all, v_all, soft_probs, rounded)

    def forward(blk_id):
        chosen, q_tile, k_all, v_all, soft_probs, rounded = block_tiles(blk_id)
        mixed_out = jnp.einsum('hqk,khd->qhd', rounded, v_all)
        return merge_heads(mixed_out).astype(jnp.bfloat16)
    attn_out = lax.map(forward, jnp.arange(BLOCKS, dtype=jnp.int32)).reshape(NODES, model_width)
    row_delta = lax.optimization_barrier(jnp.sum(split_heads(grad_out) * split_heads(attn_out), axis=2))
    delta_blocks = row_delta.reshape(BLOCKS, BLOCK, HEADS)

    def backward(state_in, blk_id):
        grad_k, grad_v = state_in
        chosen, q_tile, k_all, v_all, soft_probs, rounded = block_tiles(blk_id)
        g_tile = split_heads(g_blocks[blk_id])
        dprobs = jnp.einsum('qhd,khd->hqk', g_tile, v_all)
        dscores = soft_probs * (dprobs - delta_blocks[blk_id].T[:, :, None])
        dscores = lax.optimization_barrier(dscores.astype(jnp.bfloat16)).astype(jnp.float32)
        grad_q = jnp.einsum('hqk,khd->qhd', dscores, k_all) * factor
        dv_part = jnp.einsum('hqk,qhd->khd', rounded, g_tile).reshape(NB, BLOCK, model_width)
        dk_part = (jnp.einsum('hqk,qhd->khd', dscores, q_tile) * factor).reshape(NB, BLOCK, model_width)
        grad_k = grad_k.at[chosen].add(dk_part)
        grad_v = grad_v.at[chosen].add(dv_part)
        return ((grad_k, grad_v), merge_heads(grad_q).astype(jnp.bfloat16))
    zeros_all = jnp.zeros((BLOCKS, BLOCK, model_width), jnp.float32)
    (grad_k, grad_v), grad_q = lax.scan(backward, (zeros_all, zeros_all), jnp.arange(BLOCKS, dtype=jnp.int32))
    grad_query = grad_q.reshape(NODES, model_width)
    grad_key = grad_k.reshape(NODES, model_width).astype(jnp.bfloat16)
    grad_value = grad_v.reshape(NODES, model_width).astype(jnp.bfloat16)
    return (attn_out, grad_query, grad_key, grad_value)
```

```python
import functools
import math

import jax
import jax.numpy as jnp
from jax import lax
from jax.experimental import pallas as pl
from jax.experimental.pallas import tpu as pltpu
from jax.sharding import PartitionSpec as P

HEADS = 16
LANES = 128
F32 = jnp.float32
BF16 = jnp.bfloat16
VMEM = pl.BlockSpec(memory_space=pltpu.VMEM)
SMEM = pl.BlockSpec(memory_space=pltpu.SMEM)


def permuted(x, target):
    length = lax.axis_size("blk")
    return lax.ppermute(x, "blk", [(i, target(i) % length) for i in range(length)])


def core_swap(x):
    return permuted(x, lambda i: i ^ 1)


def pair_swap(x):
    return permuted(x, lambda i: i ^ 2)


def relay(x, sign):
    return permuted(x, lambda i: i + sign * 4 if (i & 2) == 0 else i - sign * 4)


def dot(a, b):
    return jnp.dot(a, b, preferred_element_type=F32)


def pack_body(core_ref, a_ref, b_ref, keep_ref, send_ref):
    core = core_ref[0]
    chunks, _, rows, lanes = keep_ref.shape
    half = chunks * lanes
    for index, ref in enumerate((a_ref, b_ref)):
        for chunk in range(chunks):
            mine = pl.multiple_of(core * half + chunk * lanes, lanes)
            other = pl.multiple_of((1 - core) * half + chunk * lanes, lanes)
            keep_ref[chunk, index] = ref[:, pl.ds(mine, lanes)]
            send_ref[chunk, index] = ref[:, pl.ds(other, lanes)]


def pack(core, a, b):
    rows, width = a.shape
    chunks = width // 2 // LANES
    shape = jax.ShapeDtypeStruct((chunks, 2, rows, LANES), a.dtype)
    return pl.pallas_call(
        pack_body,
        out_shape=(shape, shape),
        in_specs=[SMEM, VMEM, VMEM],
        out_specs=(VMEM, VMEM),
        name="pack",
    )(core, a, b)


def zip_body(keep_ref, recv_ref, *out_refs):
    for chunk, out_ref in enumerate(out_refs):
        out_ref[0] = keep_ref[chunk]
        out_ref[1] = recv_ref[chunk]


def zip_chunks(keep, recv):
    shape = jax.ShapeDtypeStruct((2,) + keep.shape[1:], keep.dtype)
    return pl.pallas_call(
        zip_body,
        out_shape=(shape,) * keep.shape[0],
        in_specs=[VMEM, VMEM],
        out_specs=(VMEM,) * keep.shape[0],
        name="zip",
    )(keep, recv)


def unpack_body(core_ref, *refs):
    core = core_ref[0]
    a_ref, b_ref = refs[-2:]
    chunks = (len(refs) - 2) // 2
    lanes = refs[0].shape[2]
    half = chunks * lanes
    for index, ref in enumerate((a_ref, b_ref)):
        for chunk in range(chunks):
            mine = pl.multiple_of(core * half + chunk * lanes, lanes)
            other = pl.multiple_of((1 - core) * half + chunk * lanes, lanes)
            ref[:, pl.ds(mine, lanes)] = refs[chunk][index]
            ref[:, pl.ds(other, lanes)] = refs[chunks + chunk][index]


def unpack(core, keep, recv):
    chunks = len(keep)
    _, rows, lanes = keep[0].shape
    shape = jax.ShapeDtypeStruct((rows, 2 * chunks * lanes), keep[0].dtype)
    return pl.pallas_call(
        unpack_body,
        out_shape=(shape, shape),
        in_specs=[SMEM] + [VMEM] * (2 * chunks),
        out_specs=(VMEM, VMEM),
        name="unpack",
    )(core, *keep, *recv)


def attend_body(
    slots,
    counts,
    qg_keep,
    qg_recv,
    kv_own,
    kv_pair,
    kv_far,
    od_keep,
    od_send,
    g_own,
    g_pair,
    g_far,
    kw,
    vw,
    kt,
    vt,
    dk,
    dv,
    scores,
    expd,
    mt,
    lt,
    ot,
    dqt,
):
    blk = kw.shape[1]
    own_blocks = kv_own.shape[2] // blk
    chip_blocks = 2 * own_blocks
    list_width = slots.shape[0] // chip_blocks
    head_dim = LANES // 2
    factor = 1.0 / math.sqrt(head_dim)
    for buf, ref in enumerate((kv_own, kv_pair, kv_far)):
        for src in range(2):
            for b in range(own_blocks):
                index = buf * chip_blocks + src * own_blocks + b
                k_tile = ref[src, 0, b * blk : (b + 1) * blk, :]
                v_tile = ref[src, 1, b * blk : (b + 1) * blk, :]
                kw[index] = k_tile
                vw[index] = v_tile
                kt[index] = k_tile.T
                vt[index] = v_tile.T
    dk[...] = jnp.zeros_like(dk)
    dv[...] = jnp.zeros_like(dv)
    row_ids = lax.broadcasted_iota(jnp.int32, (LANES, blk), 0)
    first_rows = row_ids < head_dim

    def lanes_first():
        return lax.broadcasted_iota(jnp.int32, (blk, LANES), 1) < head_dim

    def diagonal_t(tile_t):
        zero = jnp.zeros_like(tile_t)
        return jnp.concatenate(
            [jnp.where(first_rows, tile_t, zero), jnp.where(first_rows, zero, tile_t)], axis=1
        )

    def diagonal(tile):
        zero = jnp.zeros_like(tile)
        first = lanes_first()
        return jnp.concatenate([jnp.where(first, tile, zero), jnp.where(first, zero, tile)], axis=0)

    def collapse(wide):
        return jnp.where(first_rows, wide[:, :blk], wide[:, blk:])

    for row_block in range(chip_blocks):
        src, b = divmod(row_block, own_blocks)
        source = (qg_keep, qg_recv)[src]
        rows = slice(b * blk, (b + 1) * blk)
        q_tile = source[0, 0, rows, :].astype(F32) * factor
        g_tile = source[0, 1, rows, :].astype(F32)
        q_diag_t = diagonal_t(q_tile.T).astype(BF16)
        q_diag = diagonal(q_tile).astype(BF16)
        g_diag_t = diagonal_t(g_tile.T)
        count = counts[row_block]
        names = [slots[row_block * list_width + s] for s in range(list_width)]

        def gated(j, body):
            if j == 0:
                body()
            else:
                pl.when(2 * j < count)(body)

        def score_step(j):
            def body():
                s0, s1 = names[2 * j], names[2 * j + 1]
                top = dot(kw[s0], q_diag_t)
                low = dot(kw[s1], q_diag_t)
                low = jnp.where(2 * j + 1 < count, low, -jnp.inf)
                scores[j, :blk] = top
                scores[j, blk:] = low
                both = jnp.maximum(top, low).reshape(blk // 8, 8, 2 * blk)
                best = jnp.max(both, axis=0)
                mt[...] = best if j == 0 else jnp.maximum(mt[...], best)

            return body

        for j in range(list_width // 2):
            gated(j, score_step(j))
        row_max = jnp.max(mt[...], axis=0, keepdims=True)

        def value_step(j):
            def body():
                s0, s1 = names[2 * j], names[2 * j + 1]
                e = jnp.exp(scores[j] - row_max)
                part = jnp.sum(e.reshape(2 * blk // 8, 8, 2 * blk), axis=0)
                lt[...] = part if j == 0 else lt[...] + part
                e_bf = e.astype(BF16)
                expd[j] = e_bf
                v_t = jnp.concatenate([vt[s0], vt[s1]], axis=1)
                mixed = dot(v_t, e_bf)
                ot[...] = mixed if j == 0 else ot[...] + mixed

            return body

        for j in range(list_width // 2):
            gated(j, value_step(j))
        inverse = 1.0 / jnp.sum(lt[...], axis=0, keepdims=True)
        out_t = ot[...] * inverse
        out_rounded = out_t.astype(BF16).astype(F32)
        g_scaled_t = g_diag_t * inverse
        delta = jnp.sum(g_scaled_t * out_rounded, axis=0, keepdims=True)
        g_t_bf = g_scaled_t.astype(BF16)
        g_bf = g_scaled_t.T.astype(BF16)
        out_ref = (od_keep, od_send)[src]
        out_ref[0, rows, :] = collapse(out_t).T.astype(BF16)

        def grad_step(j):
            def body():
                s0, s1 = names[2 * j], names[2 * j + 1]
                e_bf = expd[j]
                v_both = jnp.concatenate([vw[s0], vw[s1]], axis=0)
                dp = dot(v_both, g_t_bf)
                ds = (e_bf.astype(F32) * (dp - delta)).astype(BF16)
                k_t = jnp.concatenate([kt[s0], kt[s1]], axis=1)
                moved = dot(k_t, ds)
                dqt[...] = moved if j == 0 else dqt[...] + moved
                dv_both = dot(e_bf, g_bf)
                dk_both = dot(ds, q_diag)
                dv[s0] += dv_both[:blk]
                dv[s1] += dv_both[blk:]
                dk[s0] += dk_both[:blk]
                dk[s1] += dk_both[blk:]

            return body

        for j in range(list_width // 2):
            gated(j, grad_step(j))
        out_ref[1, rows, :] = (collapse(dqt[...]) * factor).T.astype(BF16)

    for buf, ref in enumerate((g_own, g_pair, g_far)):
        for src in range(2):
            for b in range(own_blocks):
                index = buf * chip_blocks + src * own_blocks + b
                ref[src, 0, b * blk : (b + 1) * blk, :] = dk[index].astype(ref.dtype)
                ref[src, 1, b * blk : (b + 1) * blk, :] = dv[index].astype(ref.dtype)


def attend(chunk, slots, counts, qg_keep, qg_recv, kv_own, kv_pair, kv_far, blk):
    rows = kv_own.shape[2]
    chip_blocks = 2 * rows // blk
    window = 3 * chip_blocks
    list_width = slots.shape[0] // chip_blocks
    pairs = list_width // 2
    column = pl.BlockSpec((1, 2, rows, LANES), lambda i: (chunk, 0, 0, 0))
    whole = pl.BlockSpec((2, 2, rows, LANES), lambda i: (0, 0, 0, 0))
    flat = pl.BlockSpec((2, rows, LANES), lambda i: (0, 0, 0))
    units = chip_blocks * list_width
    return pl.pallas_call(
        attend_body,
        grid=(1,),
        out_shape=(
            jax.ShapeDtypeStruct((2, rows, LANES), BF16),
            jax.ShapeDtypeStruct((2, rows, LANES), BF16),
            jax.ShapeDtypeStruct((2, 2, rows, LANES), F32),
            jax.ShapeDtypeStruct((2, 2, rows, LANES), F32),
            jax.ShapeDtypeStruct((2, 2, rows, LANES), BF16),
        ),
        in_specs=[SMEM, SMEM, column, column, whole, whole, whole],
        out_specs=(flat, flat, whole, whole, whole),
        scratch_shapes=[
            pltpu.VMEM((window, blk, LANES), BF16),
            pltpu.VMEM((window, blk, LANES), BF16),
            pltpu.VMEM((window, LANES, blk), BF16),
            pltpu.VMEM((window, LANES, blk), BF16),
            pltpu.VMEM((window, blk, LANES), F32),
            pltpu.VMEM((window, blk, LANES), F32),
            pltpu.VMEM((pairs, 2 * blk, 2 * blk), F32),
            pltpu.VMEM((pairs, 2 * blk, 2 * blk), BF16),
            pltpu.VMEM((8, 2 * blk), F32),
            pltpu.VMEM((8, 2 * blk), F32),
            pltpu.VMEM((LANES, 2 * blk), F32),
            pltpu.VMEM((LANES, 2 * blk), F32),
        ],
        cost_estimate=pl.CostEstimate(
            flops=units * 24 * blk * blk * LANES,
            transcendentals=units * 2 * blk * blk,
            bytes_accessed=16 * rows * LANES * 4,
        ),
        name="attend",
    )(slots, counts, qg_keep, qg_recv, kv_own, kv_pair, kv_far)


def local(query, key_in, value, grad_out, neighbors, counts):
    rows, width = query.shape
    own_blocks, list_width = neighbors.shape
    blk = rows // own_blocks
    chunks = width // 2 // LANES
    shard_count = lax.axis_size("blk")
    shard_index = lax.axis_index("blk")
    core = shard_index % 2
    core_arr = core.astype(jnp.int32).reshape(1)

    kv_keep, kv_send = pack(core_arr, key_in, value)
    kv_recv = core_swap(kv_send)
    lists = jnp.concatenate([neighbors, counts[:, None]], axis=1)
    lists = jnp.concatenate([lists, core_swap(lists)], axis=0)
    qg_keep, qg_send = pack(core_arr, query, grad_out)
    qg_recv = core_swap(qg_send)

    home = lists[:, :list_width] // own_blocks
    step = jnp.mod(home // 2 - shard_index // 2 + 1, shard_count // 2)
    pair_step = jnp.where((shard_index // 2) % 2 == 0, 2, 0)
    buf = jnp.where(step == 1, 0, jnp.where(step == pair_step, 1, 2))
    place = (home % 2) ^ core
    slots = (buf * 2 + place) * own_blocks + lists[:, :list_width] % own_blocks
    slots = slots.astype(jnp.int32).reshape(-1)
    used = lists[:, list_width]

    kv_own = zip_chunks(kv_keep, kv_recv)
    kv_pair = [pair_swap(kv_own[c]) for c in range(chunks)]
    kv_far = [relay(kv_pair[c], 1) for c in range(chunks)]
    mine, theirs, grad_mine, grad_theirs = [], [], [], []
    for c in range(chunks):
        od_keep, od_send, g_own, g_pair, g_far = attend(
            c, slots, used, qg_keep, qg_recv, kv_own[c], kv_pair[c], kv_far[c], blk
        )
        mine.append(od_keep)
        theirs.append(od_send)
        back = relay(g_far, -1)
        total = (g_pair + back.astype(F32)).astype(BF16)
        back = pair_swap(total)
        total = (g_own + back.astype(F32)).astype(BF16)
        grad_mine.append(total[0])
        grad_theirs.append(total[1])
    got = core_swap(jnp.stack(theirs))
    attn_out, grad_query = unpack(core_arr, mine, [got[c] for c in range(chunks)])
    got = core_swap(jnp.stack(grad_theirs))
    grad_key, grad_value = unpack(core_arr, grad_mine, [got[c] for c in range(chunks)])
    return (attn_out, grad_query, grad_key, grad_value)


def solution(mesh):
    spec = P(("groups", "blk"), None)
    flat = P(("groups", "blk"))
    return jax.shard_map(
        local,
        mesh=mesh,
        in_specs=(spec, spec, spec, spec, spec, flat),
        out_specs=(spec, spec, spec, spec),
        check_vma=False,
    )
```

```python
import functools
import math

import jax
import jax.numpy as jnp
from jax import lax
from jax.experimental import pallas as pl
from jax.experimental.pallas import tpu as pltpu
from jax.sharding import PartitionSpec as P


LANES = 128
F32 = jnp.float32
BF16 = jnp.bfloat16
VMEM = pl.BlockSpec(memory_space=pltpu.VMEM)
SMEM = pl.BlockSpec(memory_space=pltpu.SMEM)
ANY = pl.BlockSpec(memory_space=pl.ANY)


def permuted(x, target):
    length = lax.axis_size("blk")
    return lax.ppermute(x, "blk", [(i, target(i) % length) for i in range(length)])


def core_swap(x):
    return permuted(x, lambda i: i ^ 1)


def pair_swap(x):
    return permuted(x, lambda i: i ^ 2)


def cross_swap(x):
    return permuted(x, lambda i: i ^ 3)


def relay(x, sign):
    return permuted(x, lambda i: i + sign * 4 if (i & 2) == 0 else i - sign * 4)


def dot(a, b):
    return jnp.dot(a, b, preferred_element_type=F32)


def columns(core, half, chunk, lanes):
    mine = pl.multiple_of(core * half + chunk * lanes, lanes)
    other = pl.multiple_of((1 - core) * half + chunk * lanes, lanes)
    return pl.ds(mine, lanes), pl.ds(other, lanes)


def run_copies(copies, sems):
    started = [
        pltpu.make_async_copy(source, target, sems.at[i])
        for i, (source, target) in enumerate(copies)
    ]
    for copy in started:
        copy.start()
    for copy in started:
        copy.wait()


def small(limit=4):
    return pltpu.CompilerParams(vmem_limit_bytes=limit << 20)


def pack_body(first, core_ref, a_ref, b_ref, keep_ref, send_ref, sems):
    copies = []
    for index, ref in enumerate((a_ref, b_ref)):
        for chunk in range(keep_ref.shape[0]):
            mine, other = columns(core_ref[0], ref.shape[1] // 2, first + chunk, LANES)
            copies.append((ref.at[:, mine], keep_ref.at[chunk, index]))
            copies.append((ref.at[:, other], send_ref.at[chunk, index]))
    run_copies(copies, sems)


def pack(core, a, b, first, last):
    rows = a.shape[0]
    shape = jax.ShapeDtypeStruct((last - first, 2, rows, LANES), a.dtype)
    return pl.pallas_call(
        functools.partial(pack_body, first),
        out_shape=(shape, shape),
        in_specs=[SMEM, ANY, ANY],
        out_specs=(VMEM, VMEM),
        scratch_shapes=[pltpu.SemaphoreType.DMA((4 * (last - first),))],
        compiler_params=small(),
        name="pack",
    )(
        core,
        pltpu.with_memory_space_constraint(a, pltpu.HBM),
        pltpu.with_memory_space_constraint(b, pltpu.HBM),
    )


def zip_body(keep_ref, recv_ref, *out_refs):
    for chunk, out_ref in enumerate(out_refs):
        out_ref[0] = keep_ref[chunk]
        out_ref[1] = recv_ref[chunk]


def zip_chunks(keep, recv):
    shape = jax.ShapeDtypeStruct((2,) + keep.shape[1:], keep.dtype)
    return pl.pallas_call(
        zip_body,
        out_shape=(shape,) * keep.shape[0],
        in_specs=[VMEM, VMEM],
        out_specs=(VMEM,) * keep.shape[0],
        compiler_params=small(),
        name="zip",
    )(keep, recv)


def place_body(count, first, aliased, core_ref, *refs):
    a_ref, b_ref, stage, sems = refs[-4:]
    copies = []
    for c in range(count):
        mine, other = columns(core_ref[0], a_ref.shape[1] // 2, first + c, LANES)
        for index, ref in enumerate((a_ref, b_ref)):
            if len(refs) - 4 - aliased == 2 * count:
                copies.append((refs[c].at[index], ref.at[:, mine]))
                copies.append((refs[count + c].at[index], ref.at[:, other]))
            else:
                own, own_add, cross, cross_add = refs[4 * c : 4 * c + 4]
                stage[c, 0, index] = (own[index] + own_add[index].astype(F32)).astype(BF16)
                total = cross[2 + index].astype(F32) + cross_add[index].astype(F32)
                stage[c, 1, index] = total.astype(BF16)
                copies.append((stage.at[c, 0, index], ref.at[:, mine]))
                copies.append((stage.at[c, 1, index], ref.at[:, other]))
    run_copies(copies, sems)


def place(core, pieces, count, first, width, onto=()):
    rows = pieces[0].shape[1]
    shape = jax.ShapeDtypeStruct((rows, width), BF16)
    aliases = {1 + len(pieces) + i: i for i in range(len(onto))}
    return pl.pallas_call(
        functools.partial(place_body, count, first, len(onto)),
        out_shape=(shape, shape),
        in_specs=[SMEM] + [VMEM] * len(pieces) + [ANY] * len(onto),
        out_specs=(ANY, ANY),
        scratch_shapes=[
            pltpu.VMEM((count, 2, 2, rows, LANES), BF16),
            pltpu.SemaphoreType.DMA((4 * count,)),
        ],
        input_output_aliases=aliases,
        compiler_params=small(8),
        name="place",
    )(core, *pieces, *onto)


def attend_body(
    slots,
    counts,
    qg_keep,
    qg_recv,
    *refs,
):
    kv_refs, refs = refs[:-19], refs[-19:]
    od_keep, to_partner, g_mine, g_pair, g_far = refs[:5]
    kw, vw, kt, vt, dk, dv, far, scores, expd, dscores, qd, gd, in_sems, out_sems = refs[5:]
    kv_at = []
    for ref in kv_refs:
        kv_at += [ref] if len(ref.shape) == 4 else [ref.at[0], ref.at[1]]
    blk = kw.shape[1]
    own_blocks = kv_at[0].shape[1]
    chip_blocks = 2 * own_blocks
    list_width = slots.shape[0] // chip_blocks
    head_dim = LANES // 2
    factor = 1.0 / math.sqrt(head_dim)
    places = [(buf, src) for buf in range(3) for src in range(2)]
    loads = []
    for buf, src in places:
        spot = pl.ds((buf * 2 + src) * own_blocks, own_blocks)
        for kind, window in enumerate((kw, vw)):
            loads.append(
                pltpu.make_async_copy(
                    kv_at[buf * 2 + src].at[kind],
                    window.at[spot],
                    in_sems.at[len(loads)],
                )
            )
    for load in loads:
        load.start()
    dk[...] = jnp.zeros_like(dk)
    dv[...] = jnp.zeros_like(dv)
    row_ids = lax.broadcasted_iota(jnp.int32, (LANES, blk), 0)
    first_rows = row_ids < head_dim
    first_lanes = lax.broadcasted_iota(jnp.int32, (blk, LANES), 1) < head_dim

    def diagonal_t(tile_t):
        zero = jnp.zeros_like(tile_t)
        return jnp.concatenate(
            [jnp.where(first_rows, tile_t, zero), jnp.where(first_rows, zero, tile_t)], axis=1
        )

    def collapse(wide):
        return jnp.where(first_rows, wide[:, :blk], wide[:, blk:])

    def slot(unit, s):
        return slots[unit * list_width + s]

    def gathered(window, unit, axis):
        return jnp.concatenate([window[slot(unit, s)] for s in range(list_width)], axis=axis)

    def live(unit, s):
        return s < counts[unit]

    def fold(tile, op):
        return op(tile.reshape(tile.shape[0] // 8, 8, tile.shape[1]), axis=0)

    def score_phase(unit):
        src, b = divmod(unit, own_blocks)
        rows = slice(b * blk, (b + 1) * blk)
        source = (qg_keep, qg_recv)[src]
        q_tile = source[0, 0, rows, :].astype(F32) * factor
        g_tile = source[0, 1, rows, :].astype(F32)
        q_diag = diagonal_t(q_tile.T).astype(BF16)
        qd[unit % 2] = q_diag
        gd[unit % 2] = diagonal_t(g_tile.T).astype(BF16)
        wide = dot(gathered(kw, unit, 0), q_diag)
        best = None
        for s in range(list_width):
            tile = wide[s * blk : (s + 1) * blk]
            scores[unit % 2, s] = tile
            top = fold(tile, jnp.max)
            if s >= 2:
                top = jnp.where(live(unit, s), top, -jnp.inf)
            best = top if best is None else jnp.maximum(best, top)
        return jnp.max(best, axis=0, keepdims=True)

    def value_phase(unit, row_max):
        total = None
        for s in range(list_width):
            base = row_max
            if s >= 2:
                base = jnp.where(live(unit, s), row_max, jnp.inf)
            e = jnp.exp(scores[unit % 2, s] - base)
            sums = fold(e, jnp.sum)
            total = sums if total is None else total + sums
            expd[unit % 2, s * blk : (s + 1) * blk] = e.astype(BF16)
        mixed = dot(gathered(vt, unit, 1), expd[unit % 2])
        return mixed, 1.0 / jnp.sum(total, axis=0, keepdims=True)

    def grad_phase(unit, mixed, inverse):
        q_t = qd[unit % 2].astype(F32)
        g_t = gd[unit % 2].astype(F32)
        src, b = divmod(unit, own_blocks)
        rows = slice(b * blk, (b + 1) * blk)
        out_ref = (od_keep, to_partner)[src]
        out_t = mixed * inverse
        out_ref[0, rows, :] = collapse(out_t).T.astype(BF16)
        delta = jnp.sum(g_t * out_t.astype(BF16).astype(F32), axis=0, keepdims=True)
        g_bf = (g_t * inverse).T.astype(BF16)
        q_bf = (q_t * inverse).T.astype(BF16)
        dp = dot(gathered(vw, unit, 0), gd[unit % 2])
        for s in range(list_width):
            part = slice(s * blk, (s + 1) * blk)
            e = expd[unit % 2, part].astype(F32)
            dscores[unit % 2, part] = (e * (dp[part] - delta)).astype(BF16)
        moved = dot(gathered(kt, unit, 1), dscores[unit % 2])
        dv_all = dot(expd[unit % 2], g_bf)
        for s in range(list_width):
            dv[slot(unit, s)] += dv_all[s * blk : (s + 1) * blk]
        dk_all = dot(dscores[unit % 2], q_bf)
        for s in range(list_width):
            dk[slot(unit, s)] += dk_all[s * blk : (s + 1) * blk]
        out_ref[1, rows, :] = (collapse(moved * inverse) * factor).T.astype(BF16)

    for load in loads:
        load.wait()
    for index in range(3 * chip_blocks):
        kt[index] = kw[index].T
        vt[index] = vw[index].T
    ahead = score_phase(0)
    for unit in range(chip_blocks):
        row_max = ahead
        mixed, inverse = value_phase(unit, row_max)
        if unit + 1 < chip_blocks:
            ahead = score_phase(unit + 1)
        grad_phase(unit, mixed, inverse)

    stores = []

    def store(source, target):
        stores.append(pltpu.make_async_copy(source, target, out_sems.at[len(stores)]))
        stores[-1].start()

    for buf, src in reversed(places):
        spot = pl.ds((buf * 2 + src) * own_blocks, own_blocks)
        for kind, window in enumerate((dk, dv)):
            if buf == 2:
                far[src, kind] = window[spot].astype(BF16)
                store(far.at[src, kind], g_far.at[src, kind])
            elif buf == 1:
                store(window.at[spot], g_pair.at[src, kind])
            elif src == 0:
                store(window.at[spot], g_mine.at[kind])
            else:
                to_partner[2 + kind] = window[spot].reshape(to_partner.shape[1:]).astype(BF16)
    for copy in stores:
        copy.wait()


def attend(chunk, slots, counts, qg_keep, qg_recv, kv, blk):
    rows = qg_keep.shape[2]
    own_blocks = rows // blk
    chip_blocks = 2 * own_blocks
    window = 3 * chip_blocks
    list_width = slots.shape[0] // chip_blocks
    column = pl.BlockSpec((1, 2, rows, LANES), lambda i: (chunk, 0, 0, 0))
    units = chip_blocks * list_width
    tail = (own_blocks, blk, LANES)
    kv = [x.reshape(x.shape[:-2] + tail) for x in kv]
    outs = pl.pallas_call(
        attend_body,
        grid=(1,),
        out_shape=(
            jax.ShapeDtypeStruct((2, rows, LANES), BF16),
            jax.ShapeDtypeStruct((4, rows, LANES), BF16),
            jax.ShapeDtypeStruct((2,) + tail, F32),
            jax.ShapeDtypeStruct((2, 2) + tail, F32),
            jax.ShapeDtypeStruct((2, 2) + tail, BF16),
        ),
        in_specs=[SMEM, SMEM, column, column] + [ANY] * len(kv),
        out_specs=(
            pl.BlockSpec((2, rows, LANES), lambda i: (0, 0, 0)),
            pl.BlockSpec((4, rows, LANES), lambda i: (0, 0, 0)),
            ANY,
            ANY,
            ANY,
        ),
        scratch_shapes=[
            pltpu.VMEM((window, blk, LANES), BF16),
            pltpu.VMEM((window, blk, LANES), BF16),
            pltpu.VMEM((window, LANES, blk), BF16),
            pltpu.VMEM((window, LANES, blk), BF16),
            pltpu.VMEM((window, blk, LANES), F32),
            pltpu.VMEM((window, blk, LANES), F32),
            pltpu.VMEM((2, 2) + tail, BF16),
            pltpu.VMEM((2, list_width, blk, 2 * blk), F32),
            pltpu.VMEM((2, list_width * blk, 2 * blk), BF16),
            pltpu.VMEM((2, list_width * blk, 2 * blk), BF16),
            pltpu.VMEM((2, LANES, 2 * blk), BF16),
            pltpu.VMEM((2, LANES, 2 * blk), BF16),
            pltpu.SemaphoreType.DMA((12,)),
            pltpu.SemaphoreType.DMA((10,)),
        ],
        compiler_params=pltpu.CompilerParams(vmem_limit_bytes=24 << 20),
        cost_estimate=pl.CostEstimate(
            flops=units * 24 * blk * blk * LANES,
            transcendentals=units * 2 * blk * blk,
            bytes_accessed=16 * rows * LANES * 4,
        ),
        name="attend",
    )(slots, counts, qg_keep, qg_recv, *kv)
    return tuple(x.reshape(x.shape[:-3] + (rows, LANES)) if x.ndim > 3 else x for x in outs)


def local(query, key_in, value, grad_out, neighbors, counts):
    rows, width = query.shape
    own_blocks, list_width = neighbors.shape
    blk = rows // own_blocks
    chunks = width // 2 // LANES
    shard_count = lax.axis_size("blk")
    shard_index = lax.axis_index("blk")
    core = shard_index % 2
    core_arr = core.astype(jnp.int32).reshape(1)

    keep, send = pack(core_arr, key_in, value, 0, 1)
    recv = core_swap(send)
    own = [(keep[0], recv[0])]
    pair = [(pair_swap(keep)[0], pair_swap(recv)[0])]
    keep, send = pack(core_arr, key_in, value, 1, chunks)
    recv = core_swap(send)
    own += [(x,) for x in zip_chunks(keep, recv)]
    pair += [(pair_swap(own[c][0]),) for c in range(1, chunks)]
    far = [(relay(pair[0][0], 1), relay(pair[0][1], 1))]
    far += [(relay(pair[c][0], 1),) for c in range(1, chunks)]

    lists = jnp.concatenate([neighbors, counts[:, None]], axis=1)
    lists = jnp.concatenate([lists, core_swap(lists)], axis=0)
    qg_keep, qg_send = pack(core_arr, query, grad_out, 0, chunks)
    qg_recv = core_swap(qg_send)

    home = lists[:, :list_width] // own_blocks
    step = jnp.mod(home // 2 - shard_index // 2 + 1, shard_count // 2)
    pair_step = jnp.where((shard_index // 2) % 2 == 0, 2, 0)
    buf = jnp.where(step == 1, 0, jnp.where(step == pair_step, 1, 2))
    spot = (home % 2) ^ core
    slots = (buf * 2 + spot) * own_blocks + lists[:, :list_width] % own_blocks
    slots = slots.astype(jnp.int32).reshape(-1)
    used = lists[:, list_width]

    kept, crossed, sums = [], [], []
    for c in range(chunks):
        od_keep, to_partner, g_mine, g_pair, g_far = attend(
            c, slots, used, qg_keep, qg_recv, own[c] + pair[c] + far[c], blk
        )
        kept.append(od_keep)
        crossed.append(core_swap(to_partner))
        back = relay(g_far, -1).astype(F32)
        near = pair_swap((g_pair[0] + back[0]).astype(BF16))
        cross = cross_swap((g_pair[1] + back[1]).astype(BF16))
        sums.append((g_mine, near, crossed[c], cross))
    attn_out, grad_query = place(core_arr, kept + crossed, chunks, 0, width)
    head = [x for four in sums[:-1] for x in four]
    grads = place(core_arr, head, chunks - 1, 0, width)
    grad_key, grad_value = place(core_arr, list(sums[-1]), 1, chunks - 1, width, grads)
    return (attn_out, grad_query, grad_key, grad_value)


def solution(mesh):
    spec = P(("groups", "blk"), None)
    flat = P(("groups", "blk"))

    return jax.shard_map(
        local,
        mesh=mesh,
        in_specs=(spec, spec, spec, spec, spec, flat),
        out_specs=(spec, spec, spec, spec),
        check_vma=False,
    )
```
